256 devices in a mesh: wa: 64 (over z, x, core), gy: 4 (over y).
Axes of the slice: x: 4, y: 4, z: 8, core: 2. Of those that a mesh axis runs over, the one named last changes fastest.
Arguments:
- bricks: bfloat16 [1024, 64, 4096], P('wa', None, 'gy'), may hold values from -6 to 6
- brick_coords: int32 [1024, 2], P('wa'), may hold values from 0 to 15, as said below
- counts: int32 [64], P('wa'), may hold values from 1 to 16, as said below
- green_kernel: bfloat16 [64, 2048, 2048], P('wa', 'gy'), may hold values from 0.19921875 to 4
Outputs:
- potential_hat: bfloat16 [64, 2, 2048, 2048], P('wa', None, 'gy')
The draws below stay inside these ranges and needn't reach their ends.
Inputs may be any that keep to these rules, and one draw needn't show every extreme that they name: Each owner's occupied slots are its first counts[o] slots; in every draw one owner fills all 16. `brick_coords`: column entries are below 2, z bricks below 16; the pairs of one owner's 16 slots are distinct.
All inputs are finite; a program needn't handle non-finite values.
Results may differ from the reference program's by a relative error of at most 0.0072.
Values may be sent and summed in bfloat16 or wider, within the bound.
A program may use at most 128 MiB of HBM per device.

```python
import math
import jax
import jax.numpy as jnp
from jax import lax

B = 64
BX = 16
BZ = 16
COL_DEV = 2
SLOTS = 16
NPAD = 2048
COLS = 128
BY = 8
YS = 512
KZ = 64
SLOTS_ALL = 1024


def draw_counts(key, part):
    owners = SLOTS_ALL // SLOTS
    values = jax.random.randint(key, (owners,), max(1, SLOTS // 4), SLOTS // 2 + 1, dtype=jnp.int32)
    chosen = jax.random.randint(jax.random.fold_in(key, 7), (), 0, owners, dtype=jnp.int32)
    return jnp.where(jnp.arange(owners, dtype=jnp.int32) == chosen, SLOTS, values).astype(jnp.int32)


def draw_brick_coords(key, part):
    owners = SLOTS_ALL // SLOTS
    subkeys = jax.random.split(jax.random.fold_in(key, 11), owners)
    orders = jax.vmap(lambda single: jax.random.permutation(single, COL_DEV * BZ))(subkeys)[:, :SLOTS]
    return jnp.stack([orders // BZ, orders % BZ], -1).reshape(SLOTS_ALL, 2).astype(jnp.int32)


def steps_of(rng, dims, cuts, least, largest):
    def one(axis_at, shards_of):
        draws = jax.random.uniform(jax.random.fold_in(jax.random.fold_in(rng, 6), axis_at), (shards_of,), jnp.float32, least / len(cuts), largest / len(cuts))
        return jnp.repeat(jnp.exp(draws), dims[axis_at] // shards_of).reshape((-1,) + (1,) * (len(dims) - axis_at - 1))

    level = one(*cuts[0])
    for cut in cuts[1:]:
        level = level * one(*cut)
    return level


def bell_draw(own_key, extent, deviation, bound, cuts=(), kind=jnp.bfloat16):
    values = jax.random.normal(own_key, extent, jnp.float32) * deviation
    if len(cuts) > 0:
        values = steps_of(own_key, extent, cuts, -0.22, 0.18) * values
    return jnp.clip(values, min=-bound, max=bound).astype(kind)


def setup_inputs(seed: int = 0) -> dict:
    splits = jax.random.split(jax.random.key(seed), 5)
    bricks = bell_draw(splits[0], (SLOTS_ALL, B, B * B), 1.0, 6.0, ((0, 64), (2, 4)))
    brick_coords = draw_brick_coords(jax.random.fold_in(splits[4], 71), 0)
    counts = draw_counts(jax.random.fold_in(splits[4], 71), 0)
    green_kernel = jnp.clip(jnp.exp(math.log(4.0) - 2.9996462 * jax.random.uniform(splits[3], (KZ, NPAD, NPAD), jnp.float32) ** steps_of(splits[3], (KZ, NPAD, NPAD), ((0, 64), (1, 4)), -0.2, 0.2)), 0.19921875, 4.0).astype(jnp.bfloat16)
    return dict(bricks=bricks, brick_coords=brick_coords, counts=counts, green_kernel=green_kernel)


def twiddle(positions, frequency, length, factor):
    product = positions[:, None] * frequency[None, :] % length
    angles = product.astype(jnp.float32) * (2.0 * math.pi / length)
    return ((jnp.cos(angles) * factor).astype(jnp.bfloat16), (jnp.sin(angles) * factor).astype(jnp.bfloat16))

def reference(bricks, brick_coords, counts, green_kernel):
    frequency = jnp.arange(KZ, dtype=jnp.int32)
    depth_cosine, depth_sine = twiddle(jnp.arange(B, dtype=jnp.int32), frequency, NPAD, 1.0 / math.sqrt(BZ * B))
    depth_table = jnp.concatenate([depth_cosine.T, -depth_sine.T], 0).astype(jnp.float32)
    slot_index = jnp.arange(SLOTS_ALL, dtype=jnp.int32)
    holder = slot_index // SLOTS
    alive_mask = (slot_index % SLOTS < counts[holder]).astype(jnp.float32)
    column = (holder * COL_DEV + brick_coords[:, 0]).astype(jnp.int32)
    offset = (brick_coords[:, 1] * B).astype(jnp.int32)

    def add_slot(totals, inputs):
        brick_data, target, offset_z, weight = inputs
        raw_terms = jnp.dot(depth_table, brick_data.astype(jnp.float32))
        real_part = raw_terms[:KZ]
        imag_part = raw_terms[KZ:]
        angles = (frequency * offset_z % NPAD).astype(jnp.float32) * (2.0 * math.pi / NPAD)
        cosine = jnp.cos(angles)[:, None]
        sine_part = jnp.sin(angles)[:, None]
        rotated = jnp.stack([real_part * cosine + imag_part * sine_part, imag_part * cosine - real_part * sine_part]) * weight
        return (totals.at[target].add(rotated), None)
    totals = lax.scan(add_slot, jnp.zeros((COLS, 2, KZ, B * B), jnp.float32), (bricks, column, offset, alive_mask))[0]
    spectra = totals.astype(jnp.bfloat16)
    layout = spectra.reshape(BY, BX, 2, KZ, B, B).transpose(3, 2, 0, 4, 1, 5).reshape(KZ, 2, YS, BX * B)
    across_cosine, across_sine = twiddle(jnp.arange(BX * B, dtype=jnp.int32), jnp.arange(NPAD, dtype=jnp.int32), NPAD, 1.0 / math.sqrt(BX * B))
    rows_cosine, rows_sine = twiddle(jnp.arange(YS, dtype=jnp.int32), jnp.arange(NPAD, dtype=jnp.int32), NPAD, 1.0 / math.sqrt(YS))
    across_cosine = across_cosine.astype(jnp.float32)
    across_sine = across_sine.astype(jnp.float32)
    rows_cosine = rows_cosine.astype(jnp.float32)
    rows_sine = rows_sine.astype(jnp.float32)

    def one_plane(inputs):
        slab_plane, kernel = inputs
        real_part = slab_plane[0].astype(jnp.float32)
        imag_part = slab_plane[1].astype(jnp.float32)
        across_real = (jnp.dot(real_part, across_cosine) + jnp.dot(imag_part, across_sine)).astype(jnp.bfloat16)
        across_imag = (jnp.dot(imag_part, across_cosine) - jnp.dot(real_part, across_sine)).astype(jnp.bfloat16)
        across_real, across_imag = lax.optimization_barrier((across_real, across_imag))
        across_real = across_real.astype(jnp.float32)
        across_imag = across_imag.astype(jnp.float32)
        final_real = jnp.dot(across_real.T, rows_cosine) + jnp.dot(across_imag.T, rows_sine)
        final_imag = jnp.dot(across_imag.T, rows_cosine) - jnp.dot(across_real.T, rows_sine)
        weights = kernel.astype(jnp.float32)
        return jnp.stack([weights * final_real, weights * final_imag]).astype(jnp.bfloat16)
    return lax.map(one_plane, (layout, green_kernel))
```

```python
import math

import jax
import jax.numpy as jnp
import ml_dtypes
import numpy as np
from jax import lax
from jax.sharding import PartitionSpec as P

BX = 16
BZ = 16
COL_DEV = 2


def wave(positions, frequency, length, factor):
    angles = (positions[:, None] * frequency[None, :] % length) * (2.0 * math.pi / length)
    return (np.cos(angles) * factor).astype(ml_dtypes.bfloat16), (np.sin(angles) * factor).astype(ml_dtypes.bfloat16)


def on_device(bricks, brick_coords, counts, green_kernel):
    depth_count, kx_count, length = green_kernel.shape
    owners = lax.axis_size("wa")
    groups = lax.axis_size("gy")
    depth_total = depth_count * owners
    slot_count, edge, cells = bricks.shape
    rows_brick = cells // edge
    depth_cosine, depth_sine = wave(np.arange(BZ * edge), np.arange(depth_total), length, 1.0 / math.sqrt(BZ * edge))
    table = np.concatenate([depth_cosine, (-depth_sine.astype(np.float32)).astype(ml_dtypes.bfloat16)], 1)
    table = jnp.asarray(table.reshape(BZ, edge, 2 * depth_total).transpose(0, 2, 1))
    picked = jnp.take(table, brick_coords[:, 1], axis=0)
    alive = jnp.arange(slot_count, dtype=jnp.int32) < counts[0]
    mine = (brick_coords[:, 0][None, :] == jnp.arange(COL_DEV, dtype=jnp.int32)[:, None]) & alive[None, :]
    mixing = picked[None] * mine[:, :, None, None].astype(jnp.bfloat16)
    sums = jnp.einsum("gsqz,szc->gqc", mixing, bricks, preferred_element_type=jnp.float32)
    spectra = sums.astype(jnp.bfloat16).reshape(COL_DEV, 2, depth_total, rows_brick, edge)
    spectra = spectra.transpose(2, 1, 3, 0, 4).reshape(depth_total, 2, rows_brick, COL_DEV * edge)
    arrived = lax.all_to_all(spectra, "wa", split_axis=0, concat_axis=0, tiled=True)
    wide = BX // COL_DEV
    brick_rows = owners // wide
    local_rows = brick_rows * rows_brick
    layout = arrived.reshape(brick_rows, wide, 2, rows_brick, COL_DEV * edge)
    layout = layout.transpose(2, 0, 3, 1, 4).reshape(2, local_rows, BX * edge)
    cosine, sine = wave(np.arange(BX * edge), np.arange(length), length, 1.0 / math.sqrt(BX * edge))
    negative = (-sine.astype(np.float32)).astype(ml_dtypes.bfloat16)
    both = jnp.asarray(np.stack([np.stack([cosine, sine]), np.stack([negative, cosine])], 0))
    planes = jnp.einsum("pyx,opxq->oyq", layout, both, preferred_element_type=jnp.float32).astype(jnp.bfloat16)
    regrouped = lax.all_to_all(planes, "gy", split_axis=2, concat_axis=1, tiled=True)
    every = np.arange(groups * local_rows)
    source, within = every // local_rows, every % local_rows
    global_rows = within // rows_brick * edge + source * rows_brick + within % rows_brick
    cosine, sine = wave(global_rows, np.arange(length), length, 1.0 / math.sqrt(brick_rows * edge))
    negative = (-sine.astype(np.float32)).astype(ml_dtypes.bfloat16)
    both = jnp.asarray(np.stack([np.stack([cosine, sine]), np.stack([negative, cosine])], 0))
    final = jnp.einsum("pyx,opyr->oxr", regrouped, both, preferred_element_type=jnp.float32)
    return (final * green_kernel.astype(jnp.float32)).astype(jnp.bfloat16)[None]


def solution(mesh):
    return jax.shard_map(
        on_device,
        mesh=mesh,
        in_specs=(P("wa", None, "gy"), P("wa", None), P("wa"), P("wa", "gy", None)),
        out_specs=P("wa", None, "gy", None),
        check_vma=False,
    )
```

```python
import functools
import math

import jax
import jax.numpy as jnp
import ml_dtypes
import numpy as np
from jax import lax
from jax.experimental import pallas as pl
from jax.experimental.pallas import tpu as pltpu
from jax.sharding import PartitionSpec as P

BX = 16
BZ = 16
COL_DEV = 2
MESH = pl.DeviceIdType.MESH
LANES = 128


def wave(positions, frequency, length, factor):
    angles = (positions[:, None] * frequency[None, :] % length) * (2.0 * math.pi / length)
    return np.cos(angles) * factor, np.sin(angles) * factor


def constant(array):
    return jnp.asarray(array.astype(ml_dtypes.bfloat16))


def quarter_turn(value):
    lane = lax.broadcasted_iota(jnp.int32, value.shape, value.ndim - 1) % LANES
    turned = jnp.concatenate(
        [pltpu.roll(value[:, at : at + LANES], LANES // 2, 1) for at in range(0, value.shape[1], LANES)], 1
    )
    return jnp.where(lane < LANES // 2, turned, -turned)


def exchange(
    coords, counts, bricks_hbm, depth_hbm, weave_hbm, gather_hbm, across_hbm, out,
    bricks, depth, weave, gather, across, mixing, spread, blocks, plane, parts, result,
    load_sem, send_sem, recv_sem, own_sem, send_sem2, recv_sem2, own_sem2,
):
    owners, groups = lax.axis_size("wa"), lax.axis_size("gy")
    me, my = lax.axis_index("wa"), lax.axis_index("gy")
    slots = coords.shape[0]
    wide = BX // COL_DEV
    loads = [
        pltpu.make_async_copy(source, target, load_sem.at[i])
        for i, (source, target) in enumerate(
            [(depth_hbm, depth), (bricks_hbm, bricks), (weave_hbm, weave), (gather_hbm, gather), (across_hbm, across)]
        )
    ]
    for load in loads:
        load.start()
    barrier = pltpu.get_barrier_semaphore()

    def greet(step, carry):
        pl.semaphore_signal(barrier, inc=1, device_id=((me + step) % owners, my), device_id_type=MESH)
        return carry

    lax.fori_loop(1, owners, greet, 0)
    for step in range(1, groups):
        pl.semaphore_signal(barrier, inc=1, device_id=(me, (my + step) % groups), device_id_type=MESH)

    loads[0].wait()
    lane = lax.broadcasted_iota(jnp.int32, (1, LANES), 1)
    for pair in range(slots // 2):
        first, second = 2 * pair, 2 * pair + 1
        picked = jnp.where(lane < LANES // 2, depth[coords[first, 1]], depth[coords[second, 1]])
        for column in range(COL_DEV):
            keep = [
                jnp.where(jnp.logical_and(coords[s, 0] == column, s < counts[0]), 1.0, 0.0).astype(jnp.float32)
                for s in (first, second)
            ]
            mask = jnp.where(lane < LANES // 2, keep[0], keep[1]).astype(jnp.bfloat16)
            mixing[column * LANES : (column + 1) * LANES, pair * LANES : (pair + 1) * LANES] = picked * mask
    loads[1].wait()
    loads[2].wait()
    wave_count = LANES // 2
    for quad in range(4):
        sums = jnp.dot(mixing[...], bricks[:, quad * 256 : (quad + 1) * 256], preferred_element_type=jnp.float32)
        sums = sums.astype(jnp.bfloat16)
        rows = [
            jnp.concatenate([sums[:LANES, at : at + LANES], sums[LANES:, at : at + LANES]], 1) for at in (0, LANES)
        ]
        woven = jnp.dot(jnp.concatenate(rows, 0), weave[...], preferred_element_type=jnp.float32)
        for pair in range(2):
            for part in range(2):
                for parity in range(2):
                    start = pair * LANES + part * wave_count
                    spread[pl.ds(parity * 16 + part * 8 + quad * 2 + pair, wave_count, stride=32), :] = woven[
                        start : start + wave_count, parity * LANES : (parity + 1) * LANES
                    ]
    blocks[...] = spread[...].astype(jnp.bfloat16).reshape(blocks.shape)

    def place(source):
        rows = pl.multiple_of(source // wide * 8, 8)
        columns = pl.multiple_of(source % wide * LANES, LANES)
        return plane.at[:, :, pl.ds(rows, 8), pl.ds(columns, LANES)]

    own = pltpu.make_async_copy(blocks.at[me], place(me), own_sem)
    own.start()
    pl.semaphore_wait(barrier, owners - 1 + groups - 1)

    def send(step, carry):
        target = (me + step) % owners
        pltpu.make_async_remote_copy(
            blocks.at[target], place(me), send_sem.at[step], recv_sem.at[step], (target, my), MESH
        ).start()
        return carry

    lax.fori_loop(1, owners, send, 0)
    own.wait()

    def receive(step, carry):
        source = (me + owners - step) % owners
        pltpu.make_async_remote_copy(
            blocks.at[source], place(source), send_sem.at[step], recv_sem.at[step], (source, my), MESH
        ).wait_recv()
        return carry

    lax.fori_loop(1, owners, receive, 0)
    loads[3].wait()
    loads[4].wait()
    for half in range(2):
        piece = plane[:, :, :, half * 512 : (half + 1) * 512].reshape(256, 512)
        sorted_ = jnp.dot(piece, gather[...], preferred_element_type=jnp.float32)
        turned = jnp.concatenate([sorted_[64:128], -sorted_[:64], sorted_[192:], -sorted_[128:192]], 0)
        for m in range(4):
            at = half * LANES
            parts[m, :, at : at + LANES] = sorted_[:, m * LANES : (m + 1) * LANES].astype(jnp.bfloat16)
            parts[m, :, 256 + at : 256 + at + LANES] = turned[:, m * LANES : (m + 1) * LANES].astype(jnp.bfloat16)
    chunk = 128
    chunks = across.shape[1] // chunk

    def outgoing(step, at):
        target = (my + step) % groups
        rows = pl.ds(at * chunk, chunk)
        return pltpu.make_async_remote_copy(
            result.at[target, :, rows, :],
            out.at[:, rows, pl.ds(pl.multiple_of(my * LANES, LANES), LANES)],
            send_sem2.at[step, at],
            recv_sem2.at[step, at],
            (me, target),
            MESH,
        )

    def incoming(step, at):
        source = (my + groups - step) % groups
        rows = pl.ds(at * chunk, chunk)
        return pltpu.make_async_remote_copy(
            result.at[source, :, rows, :],
            out.at[:, rows, pl.ds(pl.multiple_of(source * LANES, LANES), LANES)],
            send_sem2.at[step, at],
            recv_sem2.at[step, at],
            (me, source),
            MESH,
        )

    for at in range(chunks):
        rows = slice(at * chunk, (at + 1) * chunk)
        terms = [
            lax.dot_general(
                across[m, rows, :], parts[m], (((1,), (1,)), ((), ())), preferred_element_type=jnp.float32
            )
            for m in range(4)
        ]
        even, odd = terms[0] + terms[2], terms[1] + terms[3]
        even_less, odd_less = terms[0] - terms[2], quarter_turn(terms[1] - terms[3])
        for g, value in enumerate([even + odd, even_less + odd_less, even - odd, even_less - odd_less]):
            for parity in range(2):
                result[g, parity, rows, :] = value[:, parity * LANES : (parity + 1) * LANES].astype(jnp.bfloat16)
        for step in (2, 1, 3):
            outgoing(step, at).start()
    mine = pltpu.make_async_copy(
        result.at[my], out.at[:, :, pl.ds(pl.multiple_of(my * LANES, LANES), LANES)], own_sem2
    )
    mine.start()

    def sent(step, carry):
        target = (me + step) % owners
        pltpu.make_async_remote_copy(
            blocks.at[target], place(me), send_sem.at[step], recv_sem.at[step], (target, my), MESH
        ).wait_send()
        return carry

    lax.fori_loop(1, owners, sent, 0)
    mine.wait()
    for at in range(chunks):
        for step in (1, 3, 2):
            incoming(step, at).wait_recv()
            outgoing(step, at).wait_send()


def finish(planes, rows, green, out):
    length = green.shape[1]
    totals = []
    for parity in range(2):
        plain = planes[parity]
        stacked = jnp.concatenate([plain, quarter_turn(plain.astype(jnp.float32)).astype(jnp.bfloat16)], 0)
        totals.append(jnp.dot(stacked, rows[parity], preferred_element_type=jnp.float32))
    count = planes.shape[1]
    for side, total in enumerate([totals[0] + totals[1], totals[0] - totals[1]]):
        columns = slice(side * length // 2, (side + 1) * length // 2)
        weights = green[:, columns].astype(jnp.float32)
        out[0, :, columns] = (weights * total[:count]).astype(jnp.bfloat16)
        out[1, :, columns] = (weights * total[count:]).astype(jnp.bfloat16)


def tables(owners, groups, edge, rows_brick, length):
    depth_cosine, depth_sine = wave(np.arange(owners), np.arange(BZ * edge), length, 1.0 / math.sqrt(BZ * edge))
    depth = np.concatenate([depth_cosine, -depth_sine], 0).reshape(2 * owners, BZ, edge).transpose(1, 0, 2)
    depth = np.concatenate([depth, depth], 2)
    i = np.arange(256)
    column, parity, x = i // 128, i // 64 % 2, i % 64
    weave = np.zeros((256, 256), np.float32)
    weave[i, parity * 128 + x % 4 * 32 + column * 16 + x // 4] = 1.0
    i = np.arange(512)
    gather = np.zeros((512, 512), np.float32)
    gather[i, i % 128 // 32 * 128 + i // 128 * 32 + i % 32] = 1.0
    across = []
    for m in range(4):
        cosine, sine = wave(np.arange(length // 4), 4 * np.arange(256) + m, length, 1.0 / math.sqrt(BX * edge))
        across.append(np.concatenate([cosine, sine], 1))
    brick_rows = owners * COL_DEV // BX
    rows = []
    for parity in range(2):
        g = np.arange(groups)[:, None, None]
        by = np.arange(brick_rows)[None, :, None]
        y = (by * edge + g * rows_brick + np.arange(rows_brick // 2)[None, None, :] * 2 + parity).reshape(groups, -1)
        pieces = []
        for group in range(groups):
            pieces += list(wave(y[group], np.arange(length // 2), length, 1.0 / math.sqrt(brick_rows * edge)))
        rows.append(np.concatenate(pieces, 0))
    return constant(depth), constant(weave), constant(gather), constant(np.stack(across)), constant(np.stack(rows))


def on_device(bricks, brick_coords, counts, green_kernel):
    _, kx_count, length = green_kernel.shape
    owners = lax.axis_size("wa")
    groups = lax.axis_size("gy")
    slots, edge, cells = bricks.shape
    rows_brick = cells // edge
    depth, weave, gather, across, rows = tables(owners, groups, edge, rows_brick, length)
    anywhere = pl.BlockSpec(memory_space=pl.ANY)
    scalars = pl.BlockSpec(memory_space=pltpu.SMEM)
    half = jnp.bfloat16
    planes = pl.pallas_call(
        exchange,
        out_shape=jax.ShapeDtypeStruct((2, kx_count, groups * LANES), half),
        in_specs=[scalars, scalars] + [anywhere] * 5,
        out_specs=pl.BlockSpec(memory_space=pltpu.VMEM),
        scratch_shapes=[
            pltpu.VMEM((slots * edge, cells), half),
            pltpu.VMEM(depth.shape, half),
            pltpu.VMEM(weave.shape, half),
            pltpu.VMEM(gather.shape, half),
            pltpu.VMEM(across.shape, half),
            pltpu.VMEM((2 * LANES, slots * edge), half),
            pltpu.VMEM((owners * 32, LANES), jnp.float32),
            pltpu.VMEM((owners, 2, 2, 8, LANES), half),
            pltpu.VMEM((2, 2, 64, BX * edge), half),
            pltpu.VMEM((4, 256, 512), half),
            pltpu.VMEM((groups, 2, length // 4, LANES), half),
            pltpu.SemaphoreType.DMA((5,)),
            pltpu.SemaphoreType.DMA((owners,)),
            pltpu.SemaphoreType.DMA((owners,)),
            pltpu.SemaphoreType.DMA(()),
            pltpu.SemaphoreType.DMA((groups, 4)),
            pltpu.SemaphoreType.DMA((groups, 4)),
            pltpu.SemaphoreType.DMA(()),
        ],
        compiler_params=pltpu.CompilerParams(
            collective_id=0, has_side_effects=True, vmem_limit_bytes=32 << 20
        ),
        name="exchange",
    )(brick_coords, counts, bricks.reshape(slots * edge, cells), depth, weave, gather, across)
    block = 128
    return pl.pallas_call(
        finish,
        out_shape=jax.ShapeDtypeStruct((2, kx_count, length), half),
        grid=(kx_count // block,),
        in_specs=[
            pl.BlockSpec((2, block, groups * LANES), lambda i: (0, i, 0)),
            pl.BlockSpec(rows.shape, lambda i: (0, 0, 0), pipeline_mode=pl.Buffered(1)),
            pl.BlockSpec((block, length), lambda i: (i, 0)),
        ],
        out_specs=pl.BlockSpec((2, block, length), lambda i: (0, i, 0)),
        compiler_params=pltpu.CompilerParams(vmem_limit_bytes=24 << 20),
        name="finish",
    )(planes, rows, green_kernel.reshape(kx_count, length))[None]


def solution(mesh):
    return jax.shard_map(
        on_device,
        mesh=mesh,
        in_specs=(P("wa", None, "gy"), P("wa", None), P("wa"), P("wa", "gy", None)),
        out_specs=P("wa", None, "gy", None),
        check_vma=False,
    )
```

```python
import math

import jax
import jax.numpy as jnp
import ml_dtypes
import numpy as np
from jax import lax
from jax.experimental import pallas as pl
from jax.experimental.pallas import tpu as pltpu
from jax.sharding import PartitionSpec as P

BX = 16
BZ = 16
COL_DEV = 2
MESH = pl.DeviceIdType.MESH
LANES = 128
PLANE = 8
GROUPS = 4


def wave(positions, frequency, length, factor):
    angles = (positions[:, None] * frequency[None, :] % length) * (2.0 * math.pi / length)
    return np.cos(angles) * factor, np.sin(angles) * factor


def constant(array):
    return jnp.asarray(array.astype(ml_dtypes.bfloat16))


def parity_half(group):
    return group % 2, group // 2


def unpack(planes):
    wide = planes.astype(jnp.float32)
    lane = lax.broadcasted_iota(jnp.int32, (1, LANES), 1)
    halves = [[], []]
    for at in range(0, wide.shape[1], 2 * LANES):
        left, right = wide[:, at : at + LANES], wide[:, at + LANES : at + 2 * LANES]
        halves[0].append(jnp.where(lane < 64, left, pltpu.roll(right, 64, 1)))
        halves[1].append(jnp.where(lane < 64, pltpu.roll(left, 64, 1), right))
    return [jnp.concatenate(pieces, 1).astype(jnp.bfloat16) for pieces in halves]


def exchange(
    coords, counts, bricks_hbm, depth_hbm, weave_hbm, gather_hbm, across_hbm, rows_hbm, last, even, odd,
    bricks, depth, weave, gather, across, rows, mixing, spread, blocks, relay, plane, parts, result, arrived,
    load_sem, send_a, recv_a, own_a, send_b, recv_b, own_b, send_c, recv_c, own_c,
):
    owners, groups = lax.axis_size("wa"), lax.axis_size("gy")
    levels = owners // PLANE
    me, my = lax.axis_index("wa"), lax.axis_index("gy")
    level, spot = me // PLANE, me % PLANE
    slots = coords.shape[1]
    half_cells = bricks.shape[2]

    def load(i):
        source, target = [
            (depth_hbm, depth),
            (bricks_hbm.at[:, pl.ds(0, half_cells)], bricks.at[0]),
            (bricks_hbm.at[:, pl.ds(half_cells, half_cells)], bricks.at[1]),
            (weave_hbm, weave),
            (gather_hbm, gather),
            (across_hbm, across),
            (rows_hbm, rows),
        ][i]
        return pltpu.make_async_copy(source, target, load_sem.at[i])

    for i in (0, 1, 3, 2):
        load(i).start()
    barrier = pltpu.get_barrier_semaphore()
    for step in range(1, PLANE):
        peer = level * PLANE + (spot + step) % PLANE
        pl.semaphore_signal(barrier, inc=1, device_id=(peer, my), device_id_type=MESH)
    for step in range(1, levels):
        peer = (level + step) % levels * PLANE + spot
        pl.semaphore_signal(barrier, inc=1, device_id=(peer, my), device_id_type=MESH)
    for step in range(1, groups):
        pl.semaphore_signal(barrier, inc=1, device_id=(me, (my + step) % groups), device_id_type=MESH)

    load(0).wait()
    lane = lax.broadcasted_iota(jnp.int32, (1, LANES), 1)
    for pair in range(slots // 2):
        first, second = 2 * pair, 2 * pair + 1
        picked = jnp.where(lane < 64, depth[coords[1, first]], depth[coords[1, second]])
        for column in range(COL_DEV):
            keep = [
                jnp.where(jnp.logical_and(coords[0, s] == column, s < counts[0]), 1.0, 0.0).astype(jnp.float32)
                for s in (first, second)
            ]
            mask = jnp.where(lane < 64, keep[0], keep[1]).astype(jnp.bfloat16)
            mixing[column * LANES : (column + 1) * LANES, pair * LANES : (pair + 1) * LANES] = picked * mask

    def own_copy_a(g):
        return pltpu.make_async_copy(
            blocks.at[g, :, spot], relay.at[g, :, :, pl.ds(pl.multiple_of(spot * LANES, LANES), LANES)], own_a.at[g]
        )

    def start_a(g):
        own_copy_a(g).start()
        for step in range(1, PLANE):
            target = (spot + step) % PLANE
            pltpu.make_async_remote_copy(
                blocks.at[g, :, target],
                relay.at[g, :, :, pl.ds(pl.multiple_of(spot * LANES, LANES), LANES)],
                send_a.at[g],
                recv_a.at[g],
                (level * PLANE + target, my),
                MESH,
            ).start()

    def own_copy_b(g):
        return pltpu.make_async_copy(relay.at[g, level], plane.at[g, level], own_b.at[g])

    def forward_b(g):
        own_copy_a(g).wait()
        seven = relay.at[g, pl.ds(0, PLANE - 1)]
        pltpu.make_async_copy(seven, seven, recv_a.at[g]).wait()
        for step in (4, 3, 5, 2, 6, 1, 7):
            target = (level + step) % levels
            pltpu.make_async_remote_copy(
                relay.at[g, target],
                plane.at[g, level],
                send_b.at[g],
                recv_b.at[g],
                (target * PLANE + spot, my),
                MESH,
            ).start()
        own_copy_b(g).start()

    for half in range(2):
        load(1 + half).wait()
        sums = jnp.dot(mixing[...], bricks[half], preferred_element_type=jnp.float32).astype(jnp.bfloat16)
        if half == 0:
            load(3).wait()
        lines = [
            jnp.concatenate([sums[:LANES, at : at + LANES], sums[LANES:, at : at + LANES]], 1)
            for at in range(0, half_cells, LANES)
        ]
        woven = jnp.dot(jnp.concatenate(lines, 0), weave[...], preferred_element_type=jnp.float32)
        for parity in range(2):
            g = half * 2 + parity
            for i in range(4):
                for part in range(2):
                    start = i * LANES + part * 64
                    spread[g, pl.ds(part * 4 + i, 64, stride=8), :] = woven[
                        start : start + 64, parity * LANES : (parity + 1) * LANES
                    ]
            blocks[g] = spread[g].astype(jnp.bfloat16).reshape(levels, PLANE, 8, LANES)
        if half == 0:
            pl.semaphore_wait(barrier, PLANE - 1 + levels - 1 + groups - 1)
        start_a(half * 2)
        start_a(half * 2 + 1)
    for i in (4, 5, 6):
        load(i).start()
    parts[...] = jnp.zeros_like(parts)
    for g in range(GROUPS):
        forward_b(g)

    def landing(g, source):
        columns = pl.ds(pl.multiple_of(source * LANES, LANES), LANES)
        return last.at[:, columns] if g == GROUPS - 1 else arrived.at[g, :, columns]

    def own_copy_c(g):
        return pltpu.make_async_copy(result.at[g, my], landing(g, my), own_c.at[g])

    def transform(g):
        own_copy_b(g).wait()
        seven = plane.at[g, pl.ds(0, levels - 1)]
        pltpu.make_async_copy(seven, seven, recv_b.at[g]).wait()
        if g == 0:
            load(4).wait()
        sign = jnp.where(lax.broadcasted_iota(jnp.int32, (8, 8, 512), 1) < 4, 1.0, -1.0)
        for half in range(2):
            piece = plane[g, :, :, half * 512 : (half + 1) * 512].reshape(64, 512)
            ordered = jnp.dot(piece, gather[...], preferred_element_type=jnp.float32)
            turned = (pltpu.roll(ordered.reshape(8, 8, 512), 4, 1) * sign).reshape(64, 512)
            at = half * LANES
            for m in range(4):
                columns = slice(m * LANES, (m + 1) * LANES)
                for high in range(2):
                    where = slice(high * 64, (high + 1) * 64)
                    parts[m, where, high * 512 + at : high * 512 + at + LANES] = ordered[:, columns].astype(jnp.bfloat16)
                    parts[m, where, high * 512 + 256 + at : high * 512 + 256 + at + LANES] = turned[:, columns].astype(
                        jnp.bfloat16
                    )
        if g == 0:
            load(5).wait()
        terms = [
            lax.dot_general(across[m], parts[m], (((1,), (1,)), ((), ())), preferred_element_type=jnp.float32)
            for m in range(4)
        ]
        both, less = terms[0] + terms[2], terms[0] - terms[2]
        odd_both, odd_less = terms[1] + terms[3], terms[1] - terms[3]
        turn = jnp.where(lane % 8 < 4, pltpu.roll(odd_less, LANES - 4, 1), -pltpu.roll(odd_less, 4, 1))
        for quarter, value in enumerate([both + odd_both, less + turn, both - odd_both, less - turn]):
            result[g, quarter] = value.astype(jnp.bfloat16)
        for step in (2, 1, 3):
            target = (my + step) % groups
            pltpu.make_async_remote_copy(
                result.at[g, target], landing(g, my), send_c.at[g], recv_c.at[g], (me, target), MESH
            ).start()
        own_copy_c(g).start()

    def landed(g):
        own_copy_c(g).wait()
        three = (last if g == GROUPS - 1 else arrived.at[g]).at[:, pl.ds(0, (groups - 1) * LANES)]
        pltpu.make_async_copy(three, three, recv_c.at[g]).wait()

    def gather_rows(g):
        landed(g)
        if g == 0:
            load(6).wait()
        parity, half = parity_half(g)
        total = odd if parity else even
        for high, value in enumerate(unpack(arrived[g])):
            where = slice(high * 256, (high + 1) * 256)
            for at in range(0, total.shape[1], 512):
                term = jnp.dot(value, rows[g, :, at : at + 512], preferred_element_type=jnp.float32)
                if half:
                    term = term + total[where, at : at + 512]
                total[where, at : at + 512] = term

    transform(0)
    transform(1)
    transform(2)
    gather_rows(0)
    transform(3)
    gather_rows(1)
    gather_rows(2)
    landed(3)
    for g in range(GROUPS):
        seven = blocks.at[g, pl.ds(0, PLANE - 1)]
        pltpu.make_async_copy(seven, seven, send_a.at[g]).wait()
        seven = relay.at[g, pl.ds(0, levels - 1)]
        pltpu.make_async_copy(seven, seven, send_b.at[g]).wait()
        three = result.at[g, pl.ds(0, groups - 1)]
        pltpu.make_async_copy(three, three, send_c.at[g]).wait()


def finish(last, even, odd, rows, green, out, block, sem):
    count, length = green.shape
    chunk = block.shape[2]
    wide = length // 4
    unpacked = unpack(last[...])
    copies = []
    for at in range(count // chunk):
        where = slice(at * chunk, (at + 1) * chunk)
        offset = at * chunk % 256
        value = unpacked[at * chunk // 256][offset : offset + chunk]
        for part in range(2):
            for piece in range(2):
                columns = slice(part * length // 2 + piece * wide, part * length // 2 + (piece + 1) * wide)
                term = jnp.dot(value, rows[:, columns], preferred_element_type=jnp.float32) + odd[where, columns]
                base = even[where, columns]
                for side, total in enumerate([base + term, base - term]):
                    start = side * length // 2 + piece * wide
                    weights = green[where, start : start + wide].astype(jnp.float32)
                    block[at, part, :, start : start + wide] = (weights * total).astype(jnp.bfloat16)
        copies.append(pltpu.make_async_copy(block.at[at], out.at[:, pl.ds(at * chunk, chunk), :], sem.at[at]))
        copies[-1].start()
    for copy in copies:
        copy.wait()


def tables(owners, groups, edge, rows_brick, length):
    depth_cosine, depth_sine = wave(np.arange(owners), np.arange(BZ * edge), length, 1.0 / math.sqrt(BZ * edge))
    depth = np.concatenate([depth_cosine, -depth_sine], 0).reshape(2 * owners, BZ, edge).transpose(1, 0, 2)
    depth = np.concatenate([depth, depth], 2)
    i = np.arange(256)
    column, parity, x = i // 128, i // 64 % 2, i % 64
    weave = np.zeros((256, 256), np.float32)
    weave[i, parity * 128 + x % 4 * 32 + column * 16 + x // 4] = 1.0
    i = np.arange(512)
    gather = np.zeros((512, 512), np.float32)
    gather[i, i % 128 // 32 * 128 + i // 128 * 32 + i % 32] = 1.0
    across = []
    for m in range(4):
        cosine, sine = wave(np.arange(length // 4), 4 * np.arange(256) + m, length, 1.0 / math.sqrt(BX * edge))
        both = np.concatenate([cosine, sine], 1)
        across.append(np.concatenate([both[:256], both[256:]], 1))
    brick_rows = owners * COL_DEV // BX
    rows = []
    for group in range(GROUPS):
        parity, half = parity_half(group)
        source = np.arange(groups)[:, None, None, None]
        by = np.arange(brick_rows)[None, :, None, None]
        part = np.arange(2)[None, None, :, None]
        line = np.arange(rows_brick // 4)[None, None, None, :]
        y = by * edge + source * rows_brick + (half * (rows_brick // 4) + line) * 2 + parity + 0 * part
        cosine, sine = wave(y.reshape(-1), np.arange(length // 2), length, 1.0 / math.sqrt(brick_rows * edge))
        imaginary = (part + 0 * y).reshape(-1)[:, None] == 1
        rows.append(np.concatenate([np.where(imaginary, sine, cosine), np.where(imaginary, cosine, -sine)], 1))
    return [constant(t) for t in (depth, weave, gather, np.stack(across), np.stack(rows[:-1]), rows[-1])]


def on_device(bricks, brick_coords, counts, green_kernel):
    _, kx_count, length = green_kernel.shape
    owners = lax.axis_size("wa")
    groups = lax.axis_size("gy")
    slots, edge, cells = bricks.shape
    rows_brick = cells // edge
    levels = owners // PLANE
    depth, weave, gather, across, rows, rows_last = tables(owners, groups, edge, rows_brick, length)
    in_place = pl.BlockSpec(memory_space=pltpu.HBM)
    scalars = pl.BlockSpec(memory_space=pltpu.SMEM)
    on_chip = pl.BlockSpec(memory_space=pltpu.VMEM)
    half = jnp.bfloat16
    copies = pltpu.SemaphoreType.DMA
    pinned = [
        pltpu.with_memory_space_constraint(v, pltpu.HBM)
        for v in (brick_coords.T, bricks.reshape(slots * edge, cells), depth, weave, gather, across, rows)
    ]
    last, even, odd = pl.pallas_call(
        exchange,
        out_shape=[
            jax.ShapeDtypeStruct((kx_count // 2, groups * LANES), half),
            jax.ShapeDtypeStruct((kx_count, length), jnp.float32),
            jax.ShapeDtypeStruct((kx_count, length), jnp.float32),
        ],
        in_specs=[scalars, scalars] + [in_place] * 6,
        out_specs=[on_chip] * 3,
        scratch_shapes=[
            pltpu.VMEM((2, slots * edge, cells // 2), half),
            pltpu.VMEM(depth.shape, half),
            pltpu.VMEM(weave.shape, half),
            pltpu.VMEM(gather.shape, half),
            pltpu.VMEM(across.shape, half),
            pltpu.VMEM(rows.shape, half),
            pltpu.VMEM((2 * LANES, slots * edge), half),
            pltpu.VMEM((GROUPS, owners * 8, LANES), jnp.float32),
            pltpu.VMEM((GROUPS, levels, PLANE, 8, LANES), half),
            pltpu.VMEM((GROUPS, levels, 8, BX * edge), half),
            pltpu.VMEM((GROUPS, levels, 8, BX * edge), half),
            pltpu.VMEM((4, LANES, 1024), half),
            pltpu.VMEM((GROUPS, groups, 256, LANES), half),
            pltpu.VMEM((GROUPS - 1, 256, groups * LANES), half),
            copies((7,)),
        ]
        + [copies((GROUPS,))] * 9,
        compiler_params=pltpu.CompilerParams(collective_id=0, has_side_effects=True, vmem_limit_bytes=36 << 20),
        name="exchange",
    )(pinned[0], counts, *pinned[1:])
    chunk = 128
    return pl.pallas_call(
        finish,
        out_shape=jax.ShapeDtypeStruct((2, kx_count, length), half),
        in_specs=[on_chip] * 5,
        out_specs=in_place,
        scratch_shapes=[pltpu.VMEM((kx_count // chunk, 2, chunk, length), half), copies((kx_count // chunk,))],
        compiler_params=pltpu.CompilerParams(vmem_limit_bytes=30 << 20),
        name="finish",
    )(last, even, odd, rows_last, green_kernel.reshape(kx_count, length))[None]


def solution(mesh):
    return jax.shard_map(
        on_device,
        mesh=mesh,
        in_specs=(P("wa", None, "gy"), P("wa", None), P("wa"), P("wa", "gy", None)),
        out_specs=P("wa", None, "gy", None),
        check_vma=False,
    )
```

```python
import math

import jax
import jax.numpy as jnp
import ml_dtypes
import numpy as np
from jax import lax
from jax.experimental import pallas as pl
from jax.experimental.pallas import tpu as pltpu
from jax.sharding import PartitionSpec as P

BX = 16
BZ = 16
COL_DEV = 2
MESH = pl.DeviceIdType.MESH
LANES = 128
PLANE = 8
SPLIT = 1
LEVEL_FIRST = ()
GROUPS = 4


def wave(positions, frequency, length, factor):
    angles = (positions[:, None] * frequency[None, :] % length) * (2.0 * math.pi / length)
    return np.cos(angles) * factor, np.sin(angles) * factor


def constant(array):
    return jnp.asarray(array.astype(ml_dtypes.bfloat16))


def parity_half(group):
    return group % 2, group // 2


def unpack(planes):
    wide = planes.astype(jnp.float32)
    lane = lax.broadcasted_iota(jnp.int32, (1, LANES), 1)
    halves = [[], []]
    for at in range(0, wide.shape[1], 2 * LANES):
        left, right = wide[:, at : at + LANES], wide[:, at + LANES : at + 2 * LANES]
        halves[0].append(jnp.where(lane < 64, left, pltpu.roll(right, 64, 1)))
        halves[1].append(jnp.where(lane < 64, pltpu.roll(left, 64, 1), right))
    return [jnp.concatenate(pieces, 1).astype(jnp.bfloat16) for pieces in halves]


def exchange(
    coords_hbm, counts, bricks_hbm, depth_hbm, weave_hbm, gather_hbm, across_hbm, rows_hbm, last, even, odd,
    coords, bricks, depth, weave, gather, across, rows, mixing, spread, blocks, relay, middle, plane, parts, result, arrived,
    load_sem, send_ab, recv_ab, send_c, recv_c,
):
    owners, groups = lax.axis_size("wa"), lax.axis_size("gy")
    levels = owners // PLANE
    me, my = lax.axis_index("wa"), lax.axis_index("gy")
    level, spot = me // PLANE, me % PLANE
    slots = coords.shape[1]
    half_cells = bricks.shape[2]

    def load(i):
        source, target = [
            (depth_hbm, depth),
            (bricks_hbm.at[:, pl.ds(0, half_cells)], bricks.at[0]),
            (bricks_hbm.at[:, pl.ds(half_cells, half_cells)], bricks.at[1]),
            (weave_hbm, weave),
            (gather_hbm, gather),
            (across_hbm, across),
            (rows_hbm, rows),
            (coords_hbm, coords),
        ][i]
        return pltpu.make_async_copy(source, target, load_sem.at[i])

    def load_bricks(half):
        step = bricks.shape[1] // 4
        for at in range(0, bricks.shape[1], step):
            pltpu.make_async_copy(
                bricks_hbm.at[pl.ds(at, step), pl.ds(half * half_cells, half_cells)],
                bricks.at[half, pl.ds(at, step)],
                load_sem.at[1 + half],
            ).start()

    for i in (7, 0):
        load(i).start()
    load_bricks(0)
    load(3).start()
    load_bricks(1)
    barrier = pltpu.get_barrier_semaphore()
    for step in range(1, PLANE):
        peer = level * PLANE + (spot + step) % PLANE
        pl.semaphore_signal(barrier, inc=1, device_id=(peer, my), device_id_type=MESH)
    for step in range(1, levels):
        peer = (level + step) % levels * PLANE + spot
        pl.semaphore_signal(barrier, inc=1, device_id=(peer, my), device_id_type=MESH)
    for step in range(1, groups):
        pl.semaphore_signal(barrier, inc=1, device_id=(me, (my + step) % groups), device_id_type=MESH)

    for i in (7, 0):
        load(i).wait()
    lane = lax.broadcasted_iota(jnp.int32, (1, LANES), 1)
    for pair in range(slots // 2):
        first, second = 2 * pair, 2 * pair + 1
        picked = jnp.where(lane < 64, depth[coords[1, first]], depth[coords[1, second]])
        for column in range(COL_DEV):
            keep = [
                jnp.where(jnp.logical_and(coords[0, s] == column, s < counts[0]), 1.0, 0.0).astype(jnp.float32)
                for s in (first, second)
            ]
            mask = jnp.where(lane < 64, keep[0], keep[1]).astype(jnp.bfloat16)
            mixing[column * LANES : (column + 1) * LANES, pair * LANES : (pair + 1) * LANES] = picked * mask

    def stripe(buffer, g):
        return buffer.at[g, :, :, pl.ds(pl.multiple_of(spot * LANES, LANES), LANES)]

    def pieces(g, second):
        if (g in LEVEL_FIRST) == second:
            source = (lambda target: middle.at[:, target]) if second else (lambda target: blocks.at[g, :, target])
            return source, stripe(plane if second else relay, g), spot, PLANE, lambda t: level * PLANE + t
        if second:
            return lambda target: relay.at[g, target], plane.at[g, level], level, levels, lambda t: t * PLANE + spot
        return lambda target: blocks.at[g, target], middle.at[level], level, levels, lambda t: t * PLANE + spot

    def hop(g, second):
        source, target, mine, count, device = pieces(g, second)
        for step in (4, 3, 5, 2, 6, 1, 7):
            peer = (mine + step) % count
            pltpu.make_async_remote_copy(
                source(peer), target, send_ab.at[int(second), g], recv_ab.at[int(second), g], (device(peer), my), MESH
            ).start()
        target[...] = source(mine)[...]

    def hop_landed(g, second):
        buffer = plane.at[g] if second else middle if g in LEVEL_FIRST else relay.at[g]
        seven = buffer.at[pl.ds(0, 7)]
        pltpu.make_async_copy(seven, seven, recv_ab.at[int(second), g]).wait()

    def hop_sent(g, second):
        seven = plane.at[g, pl.ds(0, 7)]
        pltpu.make_async_copy(seven, seven, send_ab.at[int(second), g]).wait()

    def forward(g):
        hop_landed(g, False)
        hop(g, True)

    def column_sums(half):
        load(1 + half).wait()
        sums = jnp.dot(mixing[...], bricks[half], preferred_element_type=jnp.float32).astype(jnp.bfloat16)
        if half == 0:
            load(3).wait()
        lines = [
            jnp.concatenate([sums[:LANES, at : at + LANES], sums[LANES:, at : at + LANES]], 1)
            for at in range(0, half_cells, LANES)
        ]
        woven = jnp.dot(jnp.concatenate(lines, 0), weave[...], preferred_element_type=jnp.float32)
        for parity in range(2):
            g = half * 2 + parity
            for i in range(4):
                for part in range(2):
                    start = i * LANES + part * 64
                    spread[g, pl.ds(part * 4 + i, 64, stride=8), :] = woven[
                        start : start + 64, parity * LANES : (parity + 1) * LANES
                    ]
            blocks[g] = spread[g].astype(jnp.bfloat16).reshape(levels, PLANE, 8, LANES)

    def landing(g, source):
        columns = pl.ds(pl.multiple_of(source * LANES, LANES), LANES)
        return last.at[:, columns] if g == GROUPS - 1 else arrived.at[g, :, columns]

    def transform(g):
        hop_landed(g, True)
        if g == 0:
            load(4).wait()
        sign = jnp.where(lax.broadcasted_iota(jnp.int32, (8, 8, 512), 1) < 4, 1.0, -1.0)
        for half in range(2):
            piece = plane[g, :, :, half * 512 : (half + 1) * 512].reshape(64, 512)
            ordered = jnp.dot(piece, gather[...], preferred_element_type=jnp.float32)
            turned = (pltpu.roll(ordered.reshape(8, 8, 512), 4, 1) * sign).reshape(64, 512)
            at = half * LANES
            for m in range(4):
                columns = slice(m * LANES, (m + 1) * LANES)
                for high in range(2):
                    where = slice(high * 64, (high + 1) * 64)
                    parts[m, where, high * 512 + at : high * 512 + at + LANES] = ordered[:, columns].astype(jnp.bfloat16)
                    parts[m, where, high * 512 + 256 + at : high * 512 + 256 + at + LANES] = turned[:, columns].astype(
                        jnp.bfloat16
                    )
        if g == 0:
            load(5).wait()
        terms = [
            lax.dot_general(across[m], parts[m], (((1,), (1,)), ((), ())), preferred_element_type=jnp.float32)
            for m in range(4)
        ]
        both, less = terms[0] + terms[2], terms[0] - terms[2]
        odd_both, odd_less = terms[1] + terms[3], terms[1] - terms[3]
        turn = jnp.where(lane % 8 < 4, pltpu.roll(odd_less, LANES - 4, 1), -pltpu.roll(odd_less, 4, 1))
        for quarter, value in enumerate([both + odd_both, less + turn, both - odd_both, less - turn]):
            result[g, quarter] = value.astype(jnp.bfloat16)
        for step in (2, 1, 3):
            target = (my + step) % groups
            pltpu.make_async_remote_copy(
                result.at[g, target], landing(g, my), send_c.at[g], recv_c.at[g], (me, target), MESH
            ).start()
        landing(g, my)[...] = result[g, my]

    def landed(g):
        three = (last if g == GROUPS - 1 else arrived.at[g]).at[:, pl.ds(0, (groups - 1) * LANES)]
        pltpu.make_async_copy(three, three, recv_c.at[g]).wait()

    def gather_rows(g):
        landed(g)
        if g == 0:
            load(6).wait()
        parity, half = parity_half(g)
        total = odd if parity else even
        for high, value in enumerate(unpack(arrived[g])):
            where = slice(high * 256, (high + 1) * 256)
            for at in range(0, total.shape[1], 512):
                term = jnp.dot(value, rows[g, :, at : at + 512], preferred_element_type=jnp.float32)
                if half:
                    term = term + total[where, at : at + 512]
                total[where, at : at + 512] = term

    column_sums(0)
    pl.semaphore_wait(barrier, PLANE - 1 + levels - 1 + groups - 1)
    hop(0, False)
    hop(1, False)
    column_sums(1)
    forward(0)
    hop(2, False)
    hop(3, False)
    forward(1)
    for i in (4, 5, 6):
        load(i).start()
    parts[...] = jnp.zeros_like(parts)
    forward(2)
    forward(3)
    transform(0)
    transform(1)
    transform(2)
    gather_rows(0)
    transform(3)
    gather_rows(1)
    gather_rows(2)
    landed(3)
    for g in range(GROUPS):
        hop_sent(g, False)
        hop_sent(g, True)
        three = result.at[g, pl.ds(0, groups - 1)]
        pltpu.make_async_copy(three, three, send_c.at[g]).wait()


def finish(last, even, odd, rows, green, out, block, sem):
    count, length = green.shape
    chunk = block.shape[2]
    wide = length // 4
    unpacked = unpack(last[...])
    copies = []
    for at in range(count // chunk):
        where = slice(at * chunk, (at + 1) * chunk)
        offset = at * chunk % 256
        value = unpacked[at * chunk // 256][offset : offset + chunk]
        for part in range(2):
            for piece in range(2):
                columns = slice(part * length // 2 + piece * wide, part * length // 2 + (piece + 1) * wide)
                term = jnp.dot(value, rows[:, columns], preferred_element_type=jnp.float32) + odd[where, columns]
                base = even[where, columns]
                for side, total in enumerate([base + term, base - term]):
                    start = side * length // 2 + piece * wide
                    weights = green[where, start : start + wide].astype(jnp.float32)
                    block[at, part, :, start : start + wide] = (weights * total).astype(jnp.bfloat16)
        for piece in range(SPLIT):
            lines = pl.ds(piece * (chunk // SPLIT), chunk // SPLIT)
            rows_out = pl.ds(at * chunk + piece * (chunk // SPLIT), chunk // SPLIT)
            copies.append(pltpu.make_async_copy(block.at[at, :, lines], out.at[:, rows_out, :], sem.at[at, piece]))
            copies[-1].start()
    for copy in copies:
        copy.wait()


def tables(owners, groups, edge, rows_brick, length):
    depth_cosine, depth_sine = wave(np.arange(owners), np.arange(BZ * edge), length, 1.0 / math.sqrt(BZ * edge))
    depth = np.concatenate([depth_cosine, -depth_sine], 0).reshape(2 * owners, BZ, edge).transpose(1, 0, 2)
    depth = np.concatenate([depth, depth], 2)
    i = np.arange(256)
    column, parity, x = i // 128, i // 64 % 2, i % 64
    weave = np.zeros((256, 256), np.float32)
    weave[i, parity * 128 + x % 4 * 32 + column * 16 + x // 4] = 1.0
    i = np.arange(512)
    gather = np.zeros((512, 512), np.float32)
    gather[i, i % 128 // 32 * 128 + i // 128 * 32 + i % 32] = 1.0
    across = []
    for m in range(4):
        cosine, sine = wave(np.arange(length // 4), 4 * np.arange(256) + m, length, 1.0 / math.sqrt(BX * edge))
        both = np.concatenate([cosine, sine], 1)
        across.append(np.concatenate([both[:256], both[256:]], 1))
    brick_rows = owners * COL_DEV // BX
    rows = []
    for group in range(GROUPS):
        parity, half = parity_half(group)
        source = np.arange(groups)[:, None, None, None]
        by = np.arange(brick_rows)[None, :, None, None]
        part = np.arange(2)[None, None, :, None]
        line = np.arange(rows_brick // 4)[None, None, None, :]
        y = by * edge + source * rows_brick + (half * (rows_brick // 4) + line) * 2 + parity + 0 * part
        cosine, sine = wave(y.reshape(-1), np.arange(length // 2), length, 1.0 / math.sqrt(brick_rows * edge))
        imaginary = (part + 0 * y).reshape(-1)[:, None] == 1
        rows.append(np.concatenate([np.where(imaginary, sine, cosine), np.where(imaginary, cosine, -sine)], 1))
    return [constant(t) for t in (depth, weave, gather, np.stack(across), np.stack(rows[:-1]), rows[-1])]


def on_device(bricks, brick_coords, counts, green_kernel):
    _, kx_count, length = green_kernel.shape
    owners = lax.axis_size("wa")
    groups = lax.axis_size("gy")
    slots, edge, cells = bricks.shape
    rows_brick = cells // edge
    levels = owners // PLANE
    depth, weave, gather, across, rows, rows_last = tables(owners, groups, edge, rows_brick, length)
    in_place = pl.BlockSpec(memory_space=pltpu.HBM)
    scalars = pl.BlockSpec(memory_space=pltpu.SMEM)
    on_chip = pl.BlockSpec(memory_space=pltpu.VMEM)
    half = jnp.bfloat16
    copies = pltpu.SemaphoreType.DMA
    pinned = [
        pltpu.with_memory_space_constraint(v, pltpu.HBM)
        for v in (brick_coords.T, bricks.reshape(slots * edge, cells), depth, weave, gather, across, rows)
    ]
    last, even, odd = pl.pallas_call(
        exchange,
        out_shape=[
            jax.ShapeDtypeStruct((kx_count // 2, groups * LANES), half),
            jax.ShapeDtypeStruct((kx_count, length), jnp.float32),
            jax.ShapeDtypeStruct((kx_count, length), jnp.float32),
        ],
        in_specs=[in_place, scalars] + [in_place] * 6,
        out_specs=[on_chip] * 3,
        scratch_shapes=[
            pltpu.SMEM((COL_DEV, slots), jnp.int32),
            pltpu.VMEM((2, slots * edge, cells // 2), half),
            pltpu.VMEM(depth.shape, half),
            pltpu.VMEM(weave.shape, half),
            pltpu.VMEM(gather.shape, half),
            pltpu.VMEM(across.shape, half),
            pltpu.VMEM(rows.shape, half),
            pltpu.VMEM((2 * LANES, slots * edge), half),
            pltpu.VMEM((GROUPS, owners * 8, LANES), jnp.float32),
            pltpu.VMEM((GROUPS, levels, PLANE, 8, LANES), half),
            pltpu.VMEM((GROUPS, levels, 8, BX * edge), half),
            pltpu.VMEM((levels, PLANE, 8, LANES), half),
            pltpu.VMEM((GROUPS, levels, 8, BX * edge), half),
            pltpu.VMEM((4, LANES, 1024), half),
            pltpu.VMEM((GROUPS, groups, 256, LANES), half),
            pltpu.VMEM((GROUPS - 1, 256, groups * LANES), half),
            copies((8,)),
        ]
        + [copies((2, GROUPS))] * 2
        + [copies((GROUPS,))] * 2,
        compiler_params=pltpu.CompilerParams(collective_id=0, has_side_effects=True, vmem_limit_bytes=36 << 20),
        name="exchange",
    )(pinned[0], counts, *pinned[1:])
    chunk = 128
    return pl.pallas_call(
        finish,
        out_shape=jax.ShapeDtypeStruct((2, kx_count, length), half),
        in_specs=[on_chip] * 5,
        out_specs=in_place,
        scratch_shapes=[pltpu.VMEM((kx_count // chunk, 2, chunk, length), half), copies((kx_count // chunk, SPLIT))],
        compiler_params=pltpu.CompilerParams(vmem_limit_bytes=30 << 20),
        name="finish",
    )(last, even, odd, rows_last, green_kernel.reshape(kx_count, length))[None]


def solution(mesh):
    return jax.shard_map(
        on_device,
        mesh=mesh,
        in_specs=(P("wa", None, "gy"), P("wa", None), P("wa"), P("wa", "gy", None)),
        out_specs=P("wa", None, "gy", None),
        check_vma=False,
    )
```

```python
import math

import jax
import jax.numpy as jnp
import ml_dtypes
import numpy as np
from jax import lax
from jax.experimental import pallas as pl
from jax.experimental.pallas import tpu as pltpu
from jax.sharding import PartitionSpec as P

BX = 16
BZ = 16
COL_DEV = 2
MESH = pl.DeviceIdType.MESH
LANES = 128
PLANE = 8
SPLIT = 1
GROUPS = 4


def wave(positions, frequency, length, factor):
    angles = (positions[:, None] * frequency[None, :] % length) * (2.0 * math.pi / length)
    return np.cos(angles) * factor, np.sin(angles) * factor


def constant(array):
    return jnp.asarray(array.astype(ml_dtypes.bfloat16))


def parity_half(group):
    return group % 2, group // 2


def unpack(planes):
    wide = planes.astype(jnp.float32)
    lane = lax.broadcasted_iota(jnp.int32, (1, LANES), 1)
    halves = [[], []]
    for at in range(0, wide.shape[1], 2 * LANES):
        left, right = wide[:, at : at + LANES], wide[:, at + LANES : at + 2 * LANES]
        halves[0].append(jnp.where(lane < 64, left, pltpu.roll(right, 64, 1)))
        halves[1].append(jnp.where(lane < 64, pltpu.roll(left, 64, 1), right))
    return [jnp.concatenate(pieces, 1).astype(jnp.bfloat16) for pieces in halves]


def exchange(
    coords_hbm, counts, bricks_hbm, depth_hbm, weave_hbm, gather_hbm, across_hbm, rows_hbm, last, even, odd,
    coords, bricks, depth, weave, gather, across, rows, mixing, spread, blocks, paired, plane, parts, result, arrived,
    load_sem, send_p, recv_p, send_c, recv_c,
):
    owners, groups = lax.axis_size("wa"), lax.axis_size("gy")
    levels = owners // PLANE
    me, my = lax.axis_index("wa"), lax.axis_index("gy")
    level, spot = me // PLANE, me % PLANE
    across_x, core = spot // 2, spot % 2
    slots = coords.shape[1]
    half_cells = bricks.shape[2]

    def load(i):
        source, target = [
            (depth_hbm, depth),
            (bricks_hbm.at[:, pl.ds(0, half_cells)], bricks.at[0]),
            (bricks_hbm.at[:, pl.ds(half_cells, half_cells)], bricks.at[1]),
            (weave_hbm, weave),
            (gather_hbm, gather),
            (across_hbm, across),
            (rows_hbm, rows),
            (coords_hbm, coords),
        ][i]
        return pltpu.make_async_copy(source, target, load_sem.at[i])

    def load_bricks(half):
        step = bricks.shape[1] // 4
        for at in range(0, bricks.shape[1], step):
            pltpu.make_async_copy(
                bricks_hbm.at[pl.ds(at, step), pl.ds(half * half_cells, half_cells)],
                bricks.at[half, pl.ds(at, step)],
                load_sem.at[1 + half],
            ).start()

    for i in (7, 0):
        load(i).start()
    load_bricks(0)
    load(3).start()
    load_bricks(1)
    barrier = pltpu.get_barrier_semaphore()
    peer = level * PLANE + across_x * 2 + 1 - core
    pl.semaphore_signal(barrier, inc=1, device_id=(peer, my), device_id_type=MESH)
    for step in range(levels):
        for step_x in range(PLANE // 2):
            if step + step_x > 0:
                peer = (level + step) % levels * PLANE + (across_x + step_x) % (PLANE // 2) * 2 + core
                pl.semaphore_signal(barrier, inc=1, device_id=(peer, my), device_id_type=MESH)
    for step in range(1, groups):
        pl.semaphore_signal(barrier, inc=1, device_id=(me, (my + step) % groups), device_id_type=MESH)

    parts[...] = jnp.zeros_like(parts)
    for i in (7, 0):
        load(i).wait()
    lane = lax.broadcasted_iota(jnp.int32, (1, LANES), 1)
    for pair in range(slots // 2):
        first, second = 2 * pair, 2 * pair + 1
        picked = jnp.where(lane < 64, depth[coords[1, first]], depth[coords[1, second]])
        for column in range(COL_DEV):
            keep = [
                jnp.where(jnp.logical_and(coords[0, s] == column, s < counts[0]), 1.0, 0.0).astype(jnp.float32)
                for s in (first, second)
            ]
            mask = jnp.where(lane < 64, keep[0], keep[1]).astype(jnp.bfloat16)
            mixing[column * LANES : (column + 1) * LANES, pair * LANES : (pair + 1) * LANES] = picked * mask

    def half_lines(g):
        return paired.at[g, :, :, :, pl.ds(pl.multiple_of(core * LANES, LANES), LANES)]

    def core_hop(g):
        pltpu.make_async_remote_copy(
            blocks.at[g, :, :, 1 - core],
            half_lines(g),
            send_p.at[0, g],
            recv_p.at[0, g],
            (level * PLANE + across_x * 2 + 1 - core, my),
            MESH,
        ).start()
        half_lines(g)[...] = blocks[g, :, :, core]

    def core_forward(g):
        lines = paired.at[g, :, :, :, pl.ds(0, LANES)]
        pltpu.make_async_copy(lines, lines, recv_p.at[0, g]).wait()
        target = plane.at[g, level, :, pl.ds(pl.multiple_of(across_x * 2 * LANES, 2 * LANES), 2 * LANES)]
        for step_x in (2, 1, 3, 0):
            for step_z in (4, 3, 5, 2, 6, 1, 7, 0):
                if step_z + step_x > 0:
                    z, x = (level + step_z) % levels, (across_x + step_x) % (PLANE // 2)
                    pltpu.make_async_remote_copy(
                        paired.at[g, z, x], target, send_p.at[1, g], recv_p.at[1, g], (z * PLANE + x * 2 + core, my), MESH
                    ).start()
        target[...] = paired[g, level, across_x]

    def core_bytes(g):
        return spread.at[g, pl.ds(0, (owners // 2 - 1) * 8)]

    def column_sums(half):
        load(1 + half).wait()
        sums = jnp.dot(mixing[...], bricks[half], preferred_element_type=jnp.float32).astype(jnp.bfloat16)
        if half == 0:
            load(3).wait()
        lines = [
            jnp.concatenate([sums[:LANES, at : at + LANES], sums[LANES:, at : at + LANES]], 1)
            for at in range(0, half_cells, LANES)
        ]
        woven = jnp.dot(jnp.concatenate(lines, 0), weave[...], preferred_element_type=jnp.float32)
        for parity in range(2):
            g = half * 2 + parity
            for i in range(4):
                for part in range(2):
                    start = i * LANES + part * 64
                    spread[g, pl.ds(part * 4 + i, 64, stride=8), :] = woven[
                        start : start + 64, parity * LANES : (parity + 1) * LANES
                    ]
            blocks[g] = spread[g].astype(jnp.bfloat16).reshape(levels, PLANE // 2, 2, 8, LANES)

    def landing(g, source):
        columns = pl.ds(pl.multiple_of(source * LANES, LANES), LANES)
        return last.at[:, columns] if g == GROUPS - 1 else arrived.at[g, :, columns]

    def transform(g):
        pltpu.make_async_copy(core_bytes(g), core_bytes(g), recv_p.at[1, g]).wait()
        if g == 0:
            load(4).wait()
        sign = jnp.where(lax.broadcasted_iota(jnp.int32, (8, 8, 512), 1) < 4, 1.0, -1.0)
        for half in range(2):
            piece = plane[g, :, :, half * 512 : (half + 1) * 512].reshape(64, 512)
            ordered = jnp.dot(piece, gather[...], preferred_element_type=jnp.float32)
            turned = (pltpu.roll(ordered.reshape(8, 8, 512), 4, 1) * sign).reshape(64, 512)
            at = half * LANES
            for m in range(4):
                columns = slice(m * LANES, (m + 1) * LANES)
                for high in range(2):
                    where = slice(high * 64, (high + 1) * 64)
                    parts[m, where, high * 512 + at : high * 512 + at + LANES] = ordered[:, columns].astype(jnp.bfloat16)
                    parts[m, where, high * 512 + 256 + at : high * 512 + 256 + at + LANES] = turned[:, columns].astype(
                        jnp.bfloat16
                    )
        if g == 0:
            load(5).wait()
        terms = [
            lax.dot_general(across[m], parts[m], (((1,), (1,)), ((), ())), preferred_element_type=jnp.float32)
            for m in range(4)
        ]
        both, less = terms[0] + terms[2], terms[0] - terms[2]
        odd_both, odd_less = terms[1] + terms[3], terms[1] - terms[3]
        turn = jnp.where(lane % 8 < 4, pltpu.roll(odd_less, LANES - 4, 1), -pltpu.roll(odd_less, 4, 1))
        for quarter, value in enumerate([both + odd_both, less + turn, both - odd_both, less - turn]):
            result[g, quarter] = value.astype(jnp.bfloat16)
        for step in (2, 1, 3):
            target = (my + step) % groups
            pltpu.make_async_remote_copy(
                result.at[g, target], landing(g, my), send_c.at[g], recv_c.at[g], (me, target), MESH
            ).start()
        landing(g, my)[...] = result[g, my]

    def landed(g):
        three = (last if g == GROUPS - 1 else arrived.at[g]).at[:, pl.ds(0, (groups - 1) * LANES)]
        pltpu.make_async_copy(three, three, recv_c.at[g]).wait()

    def gather_rows(g):
        landed(g)
        if g == 0:
            load(6).wait()
        parity, half = parity_half(g)
        total = odd if parity else even
        for high, value in enumerate(unpack(arrived[g])):
            where = slice(high * 256, (high + 1) * 256)
            for at in range(0, total.shape[1], 512):
                term = jnp.dot(value, rows[g, :, at : at + 512], preferred_element_type=jnp.float32)
                if half:
                    term = term + total[where, at : at + 512]
                total[where, at : at + 512] = term

    column_sums(0)
    pl.semaphore_wait(barrier, 1 + owners // 2 - 1 + groups - 1)
    core_hop(0)
    core_hop(1)
    column_sums(1)
    core_hop(2)
    core_hop(3)
    for i in (4, 5, 6):
        load(i).start()
    core_forward(0)
    core_forward(1)
    core_forward(2)
    transform(0)
    core_forward(3)
    transform(1)
    transform(2)
    gather_rows(0)
    transform(3)
    gather_rows(1)
    gather_rows(2)
    landed(3)
    for g in range(GROUPS):
        lines = paired.at[g, :, :, :, pl.ds(0, LANES)]
        pltpu.make_async_copy(lines, lines, send_p.at[0, g]).wait()
        pltpu.make_async_copy(core_bytes(g), core_bytes(g), send_p.at[1, g]).wait()
        three = result.at[g, pl.ds(0, groups - 1)]
        pltpu.make_async_copy(three, three, send_c.at[g]).wait()


def finish(last, even, odd, rows, green, out, block, sem):
    count, length = green.shape
    chunk = block.shape[2]
    wide = length // 4
    unpacked = unpack(last[...])
    copies = []
    for at in range(count // chunk):
        where = slice(at * chunk, (at + 1) * chunk)
        offset = at * chunk % 256
        value = unpacked[at * chunk // 256][offset : offset + chunk]
        for part in range(2):
            for piece in range(2):
                columns = slice(part * length // 2 + piece * wide, part * length // 2 + (piece + 1) * wide)
                term = jnp.dot(value, rows[:, columns], preferred_element_type=jnp.float32) + odd[where, columns]
                base = even[where, columns]
                for side, total in enumerate([base + term, base - term]):
                    start = side * length // 2 + piece * wide
                    weights = green[where, start : start + wide].astype(jnp.float32)
                    block[at, part, :, start : start + wide] = (weights * total).astype(jnp.bfloat16)
        for piece in range(SPLIT):
            lines = pl.ds(piece * (chunk // SPLIT), chunk // SPLIT)
            rows_out = pl.ds(at * chunk + piece * (chunk // SPLIT), chunk // SPLIT)
            copies.append(pltpu.make_async_copy(block.at[at, :, lines], out.at[:, rows_out, :], sem.at[at, piece]))
            copies[-1].start()
    for copy in copies:
        copy.wait()


def tables(owners, groups, edge, rows_brick, length):
    depth_cosine, depth_sine = wave(np.arange(owners), np.arange(BZ * edge), length, 1.0 / math.sqrt(BZ * edge))
    depth = np.concatenate([depth_cosine, -depth_sine], 0).reshape(2 * owners, BZ, edge).transpose(1, 0, 2)
    depth = np.concatenate([depth, depth], 2)
    i = np.arange(256)
    column, parity, x = i // 128, i // 64 % 2, i % 64
    weave = np.zeros((256, 256), np.float32)
    weave[i, parity * 128 + x % 4 * 32 + column * 16 + x // 4] = 1.0
    i = np.arange(512)
    gather = np.zeros((512, 512), np.float32)
    gather[i, i % 128 // 32 * 128 + i // 128 * 32 + i % 32] = 1.0
    across = []
    for m in range(4):
        cosine, sine = wave(np.arange(length // 4), 4 * np.arange(256) + m, length, 1.0 / math.sqrt(BX * edge))
        both = np.concatenate([cosine, sine], 1)
        across.append(np.concatenate([both[:256], both[256:]], 1))
    brick_rows = owners * COL_DEV // BX
    rows = []
    for group in range(GROUPS):
        parity, half = parity_half(group)
        source = np.arange(groups)[:, None, None, None]
        by = np.arange(brick_rows)[None, :, None, None]
        part = np.arange(2)[None, None, :, None]
        line = np.arange(rows_brick // 4)[None, None, None, :]
        y = by * edge + source * rows_brick + (half * (rows_brick // 4) + line) * 2 + parity + 0 * part
        cosine, sine = wave(y.reshape(-1), np.arange(length // 2), length, 1.0 / math.sqrt(brick_rows * edge))
        imaginary = (part + 0 * y).reshape(-1)[:, None] == 1
        rows.append(np.concatenate([np.where(imaginary, sine, cosine), np.where(imaginary, cosine, -sine)], 1))
    return [constant(t) for t in (depth, weave, gather, np.stack(across), np.stack(rows[:-1]), rows[-1])]


def on_device(bricks, brick_coords, counts, green_kernel):
    _, kx_count, length = green_kernel.shape
    owners = lax.axis_size("wa")
    groups = lax.axis_size("gy")
    slots, edge, cells = bricks.shape
    rows_brick = cells // edge
    levels = owners // PLANE
    depth, weave, gather, across, rows, rows_last = tables(owners, groups, edge, rows_brick, length)
    in_place = pl.BlockSpec(memory_space=pltpu.HBM)
    scalars = pl.BlockSpec(memory_space=pltpu.SMEM)
    on_chip = pl.BlockSpec(memory_space=pltpu.VMEM)
    half = jnp.bfloat16
    copies = pltpu.SemaphoreType.DMA
    pinned = [
        pltpu.with_memory_space_constraint(v, pltpu.HBM)
        for v in (brick_coords.T, bricks.reshape(slots * edge, cells), depth, weave, gather, across, rows)
    ]
    last, even, odd = pl.pallas_call(
        exchange,
        out_shape=[
            jax.ShapeDtypeStruct((kx_count // 2, groups * LANES), half),
            jax.ShapeDtypeStruct((kx_count, length), jnp.float32),
            jax.ShapeDtypeStruct((kx_count, length), jnp.float32),
        ],
        in_specs=[in_place, scalars] + [in_place] * 6,
        out_specs=[on_chip] * 3,
        scratch_shapes=[
            pltpu.SMEM((COL_DEV, slots), jnp.int32),
            pltpu.VMEM((2, slots * edge, cells // 2), half),
            pltpu.VMEM(depth.shape, half),
            pltpu.VMEM(weave.shape, half),
            pltpu.VMEM(gather.shape, half),
            pltpu.VMEM(across.shape, half),
            pltpu.VMEM(rows.shape, half),
            pltpu.VMEM((2 * LANES, slots * edge), half),
            pltpu.VMEM((GROUPS, owners * 8, LANES), jnp.float32),
            pltpu.VMEM((GROUPS, levels, PLANE // 2, 2, 8, LANES), half),
            pltpu.VMEM((GROUPS, levels, PLANE // 2, 8, 2 * LANES), half),
            pltpu.VMEM((GROUPS, levels, 8, BX * edge), half),
            pltpu.VMEM((4, LANES, 1024), half),
            pltpu.VMEM((GROUPS, groups, 256, LANES), half),
            pltpu.VMEM((GROUPS - 1, 256, groups * LANES), half),
            copies((8,)),
        ]
        + [copies((2, GROUPS))] * 2
        + [copies((GROUPS,))] * 2,
        compiler_params=pltpu.CompilerParams(collective_id=0, has_side_effects=True, vmem_limit_bytes=36 << 20),
        name="exchange",
    )(pinned[0], counts, *pinned[1:])
    chunk = 128
    return pl.pallas_call(
        finish,
        out_shape=jax.ShapeDtypeStruct((2, kx_count, length), half),
        in_specs=[on_chip] * 5,
        out_specs=in_place,
        scratch_shapes=[pltpu.VMEM((kx_count // chunk, 2, chunk, length), half), copies((kx_count // chunk, SPLIT))],
        compiler_params=pltpu.CompilerParams(vmem_limit_bytes=30 << 20),
        name="finish",
    )(last, even, odd, rows_last, green_kernel.reshape(kx_count, length))[None]


def solution(mesh):
    return jax.shard_map(
        on_device,
        mesh=mesh,
        in_specs=(P("wa", None, "gy"), P("wa", None), P("wa"), P("wa", "gy", None)),
        out_specs=P("wa", None, "gy", None),
        check_vma=False,
    )
```

```python
import math

import jax
import jax.numpy as jnp
import ml_dtypes
import numpy as np
from jax import lax
from jax.experimental import pallas as pl
from jax.experimental.pallas import tpu as pltpu
from jax.sharding import PartitionSpec as P

BX = 16
BZ = 16
COL_DEV = 2
MESH = pl.DeviceIdType.MESH
LANES = 128
PLANE = 8
SPLIT = 1
GROUPS = 4


def wave(positions, frequency, length, factor):
    angles = (positions[:, None] * frequency[None, :] % length) * (2.0 * math.pi / length)
    return np.cos(angles) * factor, np.sin(angles) * factor


def constant(array):
    return jnp.asarray(array.astype(ml_dtypes.bfloat16))


def parity_half(group):
    return group % 2, group // 2


def unpack(planes):
    wide = planes.astype(jnp.float32)
    lane = lax.broadcasted_iota(jnp.int32, (1, LANES), 1)
    halves = [[], []]
    for at in range(0, wide.shape[1], 2 * LANES):
        left, right = wide[:, at : at + LANES], wide[:, at + LANES : at + 2 * LANES]
        halves[0].append(jnp.where(lane < 64, left, pltpu.roll(right, 64, 1)))
        halves[1].append(jnp.where(lane < 64, pltpu.roll(left, 64, 1), right))
    return [jnp.concatenate(pieces, 1).astype(jnp.bfloat16) for pieces in halves]


def exchange(
    coords_hbm, counts, bricks_hbm, depth_hbm, weave_hbm, gather_hbm, across_hbm, rows_hbm, last, even, odd,
    coords, bricks, depth, weave, gather, across, rows, mixing, spread, blocks, paired, plane, parts, result, arrived,
    load_sem, send_p, recv_p, send_c, recv_c,
):
    owners, groups = lax.axis_size("wa"), lax.axis_size("gy")
    levels = owners // PLANE
    me, my = lax.axis_index("wa"), lax.axis_index("gy")
    level, spot = me // PLANE, me % PLANE
    across_x, core = spot // 2, spot % 2
    slots = coords.shape[1]
    half_cells = bricks.shape[2]

    def load(i):
        source, target = [
            (depth_hbm, depth),
            (bricks_hbm.at[:, pl.ds(0, half_cells)], bricks.at[0]),
            (bricks_hbm.at[:, pl.ds(half_cells, half_cells)], bricks.at[1]),
            (weave_hbm, weave),
            (gather_hbm, gather),
            (across_hbm, across),
            (rows_hbm, rows),
            (coords_hbm, coords),
        ][i]
        return pltpu.make_async_copy(source, target, load_sem.at[i])

    def load_bricks(half):
        step = bricks.shape[1] // 4
        for at in range(0, bricks.shape[1], step):
            pltpu.make_async_copy(
                bricks_hbm.at[pl.ds(at, step), pl.ds(half * half_cells, half_cells)],
                bricks.at[half, pl.ds(at, step)],
                load_sem.at[1 + half],
            ).start()

    for i in (7, 0):
        load(i).start()
    load_bricks(0)
    load(3).start()
    load_bricks(1)
    barrier = pltpu.get_barrier_semaphore()
    peer = level * PLANE + across_x * 2 + 1 - core
    pl.semaphore_signal(barrier, inc=1, device_id=(peer, my), device_id_type=MESH)
    for step in range(levels):
        for step_x in range(PLANE // 2):
            if step + step_x > 0:
                peer = (level + step) % levels * PLANE + (across_x + step_x) % (PLANE // 2) * 2 + core
                pl.semaphore_signal(barrier, inc=1, device_id=(peer, my), device_id_type=MESH)
    for step in range(1, groups):
        pl.semaphore_signal(barrier, inc=1, device_id=(me, (my + step) % groups), device_id_type=MESH)

    parts[...] = jnp.zeros_like(parts)
    for i in (7, 0):
        load(i).wait()
    lane = lax.broadcasted_iota(jnp.int32, (1, LANES), 1)
    for pair in range(slots // 2):
        first, second = 2 * pair, 2 * pair + 1
        picked = jnp.where(lane < 64, depth[coords[1, first]], depth[coords[1, second]])
        for column in range(COL_DEV):
            keep = [
                jnp.where(jnp.logical_and(coords[0, s] == column, s < counts[0]), 1.0, 0.0).astype(jnp.float32)
                for s in (first, second)
            ]
            mask = jnp.where(lane < 64, keep[0], keep[1]).astype(jnp.bfloat16)
            mixing[column * LANES : (column + 1) * LANES, pair * LANES : (pair + 1) * LANES] = picked * mask

    def half_lines(g):
        return paired.at[g, :, :, :, pl.ds(pl.multiple_of(core * LANES, LANES), LANES)]

    def core_hop(g):
        pltpu.make_async_remote_copy(
            blocks.at[g, :, :, 1 - core],
            half_lines(g),
            send_p.at[0, g],
            recv_p.at[0, g],
            (level * PLANE + across_x * 2 + 1 - core, my),
            MESH,
        ).start()
        half_lines(g)[...] = blocks[g, :, :, core]

    def core_forward(g):
        lines = paired.at[g, :, :, :, pl.ds(0, LANES)]
        pltpu.make_async_copy(lines, lines, recv_p.at[0, g]).wait()
        target = plane.at[g, level, :, pl.ds(pl.multiple_of(across_x * 2 * LANES, 2 * LANES), 2 * LANES)]
        for step_x in (2, 1, 3, 0):
            for step_z in (4, 3, 5, 2, 6, 1, 7, 0):
                if step_z + step_x > 0:
                    z, x = (level + step_z) % levels, (across_x + step_x) % (PLANE // 2)
                    pltpu.make_async_remote_copy(
                        paired.at[g, z, x], target, send_p.at[1, g], recv_p.at[1, g], (z * PLANE + x * 2 + core, my), MESH
                    ).start()
        target[...] = paired[g, level, across_x]

    def core_bytes(g):
        return spread.at[g, pl.ds(0, (owners // 2 - 1) * 8)]

    def column_sums(half):
        load(1 + half).wait()
        sums = jnp.dot(mixing[...], bricks[half], preferred_element_type=jnp.float32).astype(jnp.bfloat16)
        if half == 0:
            load(3).wait()
        lines = [
            jnp.concatenate([sums[:LANES, at : at + LANES], sums[LANES:, at : at + LANES]], 1)
            for at in range(0, half_cells, LANES)
        ]
        woven = jnp.dot(jnp.concatenate(lines, 0), weave[...], preferred_element_type=jnp.float32)
        for parity in range(2):
            g = half * 2 + parity
            for i in range(4):
                for part in range(2):
                    start = i * LANES + part * 64
                    spread[g, pl.ds(part * 4 + i, 64, stride=8), :] = woven[
                        start : start + 64, parity * LANES : (parity + 1) * LANES
                    ]
            blocks[g] = spread[g].astype(jnp.bfloat16).reshape(levels, PLANE // 2, 2, 8, LANES)

    def landing(g, source):
        columns = pl.ds(pl.multiple_of(source * LANES, LANES), LANES)
        return last.at[:, columns] if g == GROUPS - 1 else arrived.at[g, :, columns]

    def transform(g):
        pltpu.make_async_copy(core_bytes(g), core_bytes(g), recv_p.at[1, g]).wait()
        if g == 0:
            load(4).wait()
        sign = jnp.where(lax.broadcasted_iota(jnp.int32, (8, 8, 512), 1) < 4, 1.0, -1.0)
        for half in range(2):
            piece = plane[g, :, :, half * 512 : (half + 1) * 512].reshape(64, 512)
            ordered = jnp.dot(piece, gather[...], preferred_element_type=jnp.float32)
            turned = (pltpu.roll(ordered.reshape(8, 8, 512), 4, 1) * sign).reshape(64, 512)
            at = half * LANES
            for m in range(4):
                columns = slice(m * LANES, (m + 1) * LANES)
                for high in range(2):
                    where = slice(high * 64, (high + 1) * 64)
                    parts[m, where, high * 512 + at : high * 512 + at + LANES] = ordered[:, columns].astype(jnp.bfloat16)
                    parts[m, where, high * 512 + 256 + at : high * 512 + 256 + at + LANES] = turned[:, columns].astype(
                        jnp.bfloat16
                    )
        if g == 0:
            load(5).wait()
        terms = [
            lax.dot_general(across[m], parts[m], (((1,), (1,)), ((), ())), preferred_element_type=jnp.float32)
            for m in range(4)
        ]
        both, less = terms[0] + terms[2], terms[0] - terms[2]
        odd_both, odd_less = terms[1] + terms[3], terms[1] - terms[3]
        turn = jnp.where(lane % 8 < 4, pltpu.roll(odd_less, LANES - 4, 1), -pltpu.roll(odd_less, 4, 1))
        for quarter, value in enumerate([both + odd_both, less + turn, both - odd_both, less - turn]):
            result[g, quarter] = value.astype(jnp.bfloat16)
        for step in (1, 3, 2):
            target = (my + step) % groups
            pltpu.make_async_remote_copy(
                result.at[g, target], landing(g, my), send_c.at[g], recv_c.at[g], (me, target), MESH
            ).start()
        landing(g, my)[...] = result[g, my]

    def landed(g):
        three = (last if g == GROUPS - 1 else arrived.at[g]).at[:, pl.ds(0, (groups - 1) * LANES)]
        pltpu.make_async_copy(three, three, recv_c.at[g]).wait()

    def gather_rows(g):
        landed(g)
        if g == 0:
            load(6).wait()
        parity, half = parity_half(g)
        total = odd if parity else even
        for high, value in enumerate(unpack(arrived[g])):
            where = slice(high * 256, (high + 1) * 256)
            for at in range(0, total.shape[1], 512):
                term = jnp.dot(value, rows[g, :, at : at + 512], preferred_element_type=jnp.float32)
                if half:
                    term = term + total[where, at : at + 512]
                total[where, at : at + 512] = term

    column_sums(0)
    pl.semaphore_wait(barrier, 1 + owners // 2 - 1 + groups - 1)
    core_hop(0)
    core_hop(1)
    column_sums(1)
    core_hop(2)
    core_hop(3)
    for i in (4, 5, 6):
        load(i).start()
    core_forward(0)
    core_forward(1)
    core_forward(2)
    transform(0)
    core_forward(3)
    transform(1)
    transform(2)
    gather_rows(0)
    transform(3)
    gather_rows(1)
    gather_rows(2)
    landed(3)
    for g in range(GROUPS):
        lines = paired.at[g, :, :, :, pl.ds(0, LANES)]
        pltpu.make_async_copy(lines, lines, send_p.at[0, g]).wait()
        pltpu.make_async_copy(core_bytes(g), core_bytes(g), send_p.at[1, g]).wait()
        three = result.at[g, pl.ds(0, groups - 1)]
        pltpu.make_async_copy(three, three, send_c.at[g]).wait()


def finish(last, even, odd, rows, green, out, block, sem):
    count, length = green.shape
    chunk = block.shape[2]
    wide = length // 4
    unpacked = unpack(last[...])
    copies = []
    for at in range(count // chunk):
        where = slice(at * chunk, (at + 1) * chunk)
        offset = at * chunk % 256
        value = unpacked[at * chunk // 256][offset : offset + chunk]
        for part in range(2):
            for piece in range(2):
                columns = slice(part * length // 2 + piece * wide, part * length // 2 + (piece + 1) * wide)
                term = jnp.dot(value, rows[:, columns], preferred_element_type=jnp.float32) + odd[where, columns]
                base = even[where, columns]
                for side, total in enumerate([base + term, base - term]):
                    start = side * length // 2 + piece * wide
                    weights = green[where, start : start + wide].astype(jnp.float32)
                    block[at, part, :, start : start + wide] = (weights * total).astype(jnp.bfloat16)
        for piece in range(SPLIT):
            lines = pl.ds(piece * (chunk // SPLIT), chunk // SPLIT)
            rows_out = pl.ds(at * chunk + piece * (chunk // SPLIT), chunk // SPLIT)
            copies.append(pltpu.make_async_copy(block.at[at, :, lines], out.at[:, rows_out, :], sem.at[at, piece]))
            copies[-1].start()
    for copy in copies:
        copy.wait()


def tables(owners, groups, edge, rows_brick, length):
    depth_cosine, depth_sine = wave(np.arange(owners), np.arange(BZ * edge), length, 1.0 / math.sqrt(BZ * edge))
    depth = np.concatenate([depth_cosine, -depth_sine], 0).reshape(2 * owners, BZ, edge).transpose(1, 0, 2)
    depth = np.concatenate([depth, depth], 2)
    i = np.arange(256)
    column, parity, x = i // 128, i // 64 % 2, i % 64
    weave = np.zeros((256, 256), np.float32)
    weave[i, parity * 128 + x % 4 * 32 + column * 16 + x // 4] = 1.0
    i = np.arange(512)
    gather = np.zeros((512, 512), np.float32)
    gather[i, i % 128 // 32 * 128 + i // 128 * 32 + i % 32] = 1.0
    across = []
    for m in range(4):
        cosine, sine = wave(np.arange(length // 4), 4 * np.arange(256) + m, length, 1.0 / math.sqrt(BX * edge))
        both = np.concatenate([cosine, sine], 1)
        across.append(np.concatenate([both[:256], both[256:]], 1))
    brick_rows = owners * COL_DEV // BX
    rows = []
    for group in range(GROUPS):
        parity, half = parity_half(group)
        source = np.arange(groups)[:, None, None, None]
        by = np.arange(brick_rows)[None, :, None, None]
        part = np.arange(2)[None, None, :, None]
        line = np.arange(rows_brick // 4)[None, None, None, :]
        y = by * edge + source * rows_brick + (half * (rows_brick // 4) + line) * 2 + parity + 0 * part
        cosine, sine = wave(y.reshape(-1), np.arange(length // 2), length, 1.0 / math.sqrt(brick_rows * edge))
        imaginary = (part + 0 * y).reshape(-1)[:, None] == 1
        rows.append(np.concatenate([np.where(imaginary, sine, cosine), np.where(imaginary, cosine, -sine)], 1))
    return [constant(t) for t in (depth, weave, gather, np.stack(across), np.stack(rows[:-1]), rows[-1])]


def on_device(bricks, brick_coords, counts, green_kernel):
    _, kx_count, length = green_kernel.shape
    owners = lax.axis_size("wa")
    groups = lax.axis_size("gy")
    slots, edge, cells = bricks.shape
    rows_brick = cells // edge
    levels = owners // PLANE
    depth, weave, gather, across, rows, rows_last = tables(owners, groups, edge, rows_brick, length)
    in_place = pl.BlockSpec(memory_space=pltpu.HBM)
    scalars = pl.BlockSpec(memory_space=pltpu.SMEM)
    on_chip = pl.BlockSpec(memory_space=pltpu.VMEM)
    half = jnp.bfloat16
    copies = pltpu.SemaphoreType.DMA
    pinned = [
        pltpu.with_memory_space_constraint(v, pltpu.HBM)
        for v in (brick_coords.T, bricks.reshape(slots * edge, cells), depth, weave, gather, across, rows)
    ]
    last, even, odd = pl.pallas_call(
        exchange,
        out_shape=[
            jax.ShapeDtypeStruct((kx_count // 2, groups * LANES), half),
            jax.ShapeDtypeStruct((kx_count, length), jnp.float32),
            jax.ShapeDtypeStruct((kx_count, length), jnp.float32),
        ],
        in_specs=[in_place, scalars] + [in_place] * 6,
        out_specs=[on_chip] * 3,
        scratch_shapes=[
            pltpu.SMEM((COL_DEV, slots), jnp.int32),
            pltpu.VMEM((2, slots * edge, cells // 2), half),
            pltpu.VMEM(depth.shape, half),
            pltpu.VMEM(weave.shape, half),
            pltpu.VMEM(gather.shape, half),
            pltpu.VMEM(across.shape, half),
            pltpu.VMEM(rows.shape, half),
            pltpu.VMEM((2 * LANES, slots * edge), half),
            pltpu.VMEM((GROUPS, owners * 8, LANES), jnp.float32),
            pltpu.VMEM((GROUPS, levels, PLANE // 2, 2, 8, LANES), half),
            pltpu.VMEM((GROUPS, levels, PLANE // 2, 8, 2 * LANES), half),
            pltpu.VMEM((GROUPS, levels, 8, BX * edge), half),
            pltpu.VMEM((4, LANES, 1024), half),
            pltpu.VMEM((GROUPS, groups, 256, LANES), half),
            pltpu.VMEM((GROUPS - 1, 256, groups * LANES), half),
            copies((8,)),
        ]
        + [copies((2, GROUPS))] * 2
        + [copies((GROUPS,))] * 2,
        compiler_params=pltpu.CompilerParams(collective_id=0, has_side_effects=True, vmem_limit_bytes=36 << 20),
        name="exchange",
    )(pinned[0], counts, *pinned[1:])
    chunk = 128
    return pl.pallas_call(
        finish,
        out_shape=jax.ShapeDtypeStruct((2, kx_count, length), half),
        in_specs=[on_chip] * 5,
        out_specs=in_place,
        scratch_shapes=[pltpu.VMEM((kx_count // chunk, 2, chunk, length), half), copies((kx_count // chunk, SPLIT))],
        compiler_params=pltpu.CompilerParams(vmem_limit_bytes=30 << 20),
        name="finish",
    )(last, even, odd, rows_last, green_kernel.reshape(kx_count, length))[None]


def solution(mesh):
    return jax.shard_map(
        on_device,
        mesh=mesh,
        in_specs=(P("wa", None, "gy"), P("wa", None), P("wa"), P("wa", "gy", None)),
        out_specs=P("wa", None, "gy", None),
        check_vma=False,
    )
```
